32 devices in a mesh: seq: 16 (over z, y, x), chan: 2 (over core).
Axes of the slice: x: 2, y: 2, z: 4, core: 2. Of those that a mesh axis runs over, the one named last changes fastest.
Arguments:
- x_in: bfloat16 [32768, 2048], P('seq', 'chan'), may hold values from -6 to 6
- gate_in: bfloat16 [32768, 2048], P('seq', 'chan'), may hold values from -70 to 70
- b_in: bfloat16 [32768, 64], P('seq'), may hold values from -0.75 to 0.75
- c_in: bfloat16 [32768, 64], P('seq'), may hold values from -6 to 6
- step_size: float32 [32, 32768], P('chan', 'seq'), may hold values from 0 to 1, as said below
- log_keep: float32 [32, 32768], P('chan', 'seq'), may hold values from -2 to 0
- skip_gain: float32 [32], P('chan'), may hold values from 0.5 to 1.5
- norm_gain: float32 [2048], P('chan'), may hold values from 0.25 to 1.75
Outputs:
- mixed: bfloat16 [32768, 2048], P('seq', 'chan')
The draws below stay inside these ranges and needn't reach their ends.
Inputs may be any that keep to these rules, and one draw needn't show every extreme that they name: `step_size`: positive.
All inputs are finite; a program needn't handle non-finite values.
Results may differ from the reference program's by a relative error of at most 0.005.
Values sent between devices are 32-bit elements; how exact they have to be, the bound alone decides.
A program may use at most 64 MiB of HBM per device.

```python
import math
import jax
import jax.numpy as jnp
from jax import lax

CH = 2048
HEADDIM = 64
STATE = 64
BLOCK = 256
TOK_DEV = 2048
HEADS = 32
SEQUENCE_TOKENS = 32768


def decay_pieces(key):
    random_subkeys = jax.random.split(jax.random.fold_in(key, 17), 7)
    ranking = jax.random.permutation(random_subkeys[0], HEADS)
    slow_count = max(HEADS // 2, 1)
    is_slow = ranking < slow_count
    slow_rate = jnp.exp(jax.random.uniform(random_subkeys[1], (HEADS,), jnp.float32, math.log(0.2), math.log(0.5))) / SEQUENCE_TOKENS
    fast_rate = jnp.exp(jax.random.uniform(random_subkeys[2], (HEADS,), jnp.float32, math.log(0.02), math.log(0.05)))
    head_decay_rate = jnp.where(is_slow, slow_rate, fast_rate)
    token_multiplier = jnp.exp(jax.random.uniform(random_subkeys[3], (HEADS, SEQUENCE_TOKENS), jnp.float32, math.log(0.5), math.log(2.0)))
    device_multiplier = jnp.exp(jax.random.uniform(random_subkeys[4], (HEADS, SEQUENCE_TOKENS // TOK_DEV), jnp.float32, math.log(0.5), math.log(2.0)))
    device_multiplier = jnp.repeat(device_multiplier, TOK_DEV, axis=1)
    spike_position = jax.random.randint(random_subkeys[5], (2,), 0, SEQUENCE_TOKENS)
    spike_fraction = jax.random.uniform(random_subkeys[6], (2,), jnp.float32, 0.2, 0.5)
    token_positions = jnp.arange(SEQUENCE_TOKENS, dtype=jnp.int32)
    spike_amount = jnp.sum(jnp.where(token_positions[None, :] == spike_position[:, None], jnp.log(1.0 - spike_fraction)[:, None], 0.0), axis=0)
    return (head_decay_rate, head_decay_rate[:, None] * token_multiplier * device_multiplier, spike_amount)


def draw_log_keep(key, part):
    head_decay_rate, token_level, spike_amount = decay_pieces(key)
    return (spike_amount[None, :] - token_level).astype(jnp.float32)


def draw_step_size(key, part):
    head_decay_rate, token_level, spike_amount = decay_pieces(key)
    factor = jnp.exp(jax.random.uniform(jax.random.fold_in(key, 29), (HEADS, SEQUENCE_TOKENS), jnp.float32, math.log(0.5), math.log(2.0)))
    return (jnp.sqrt(2.0 * head_decay_rate)[:, None] * factor).astype(jnp.float32)


def draw_gate_in(key, part):
    random_subkeys = jax.random.split(jax.random.fold_in(key, 5), 2)
    column = jnp.arange(CH, dtype=jnp.float32) / max(CH - 1, 1)
    col_scale = jnp.sqrt(3.0) ** column * jnp.exp(jax.random.uniform(random_subkeys[0], (CH,), jnp.float32, 0.0, math.log(10.0)))
    noise_base = jnp.clip(jax.random.normal(random_subkeys[1], (SEQUENCE_TOKENS, CH), jnp.float32), -4.0, 4.0)
    return (noise_base * col_scale[None, :]).astype(jnp.bfloat16)


def steps_of(own_key, extent, shards, least, top_value):
    gain = 1.0
    for position, blocks in shards:
        steps = jax.random.uniform(jax.random.fold_in(jax.random.fold_in(own_key, 6), position), (blocks,), jnp.float32, least / len(shards), top_value / len(shards))
        gain = gain * jnp.repeat(jnp.exp(steps), extent[position] // blocks).reshape((-1,) + (1,) * (len(extent) - 1 - position))
    return gain


def noise(rng, dims, deviation, limit, cuts=(), kind=jnp.bfloat16):
    result = jax.random.normal(rng, dims, jnp.float32) * deviation
    if len(cuts) > 0:
        result = steps_of(rng, dims, cuts, -0.22, 0.18) * result
    return jnp.clip(result, min=-limit, max=limit).astype(kind)


def setup_inputs(seed: int = 0) -> dict:
    seeds = jax.random.split(jax.random.key(seed), 9)
    return {
        "x_in": noise(seeds[0], (SEQUENCE_TOKENS, CH), 1.0, 6.0, ((0, 16), (1, 2))),
        "gate_in": draw_gate_in(jax.random.fold_in(seeds[8], 71), 0),
        "b_in": noise(seeds[2], (SEQUENCE_TOKENS, STATE), STATE ** -0.5, 0.75, ((0, 16),)),
        "c_in": noise(seeds[3], (SEQUENCE_TOKENS, STATE), 1.0, 6.0, ((0, 16),)),
        "step_size": draw_step_size(jax.random.fold_in(seeds[8], 71), 0),
        "log_keep": draw_log_keep(jax.random.fold_in(seeds[8], 71), 0),
        "skip_gain": jnp.clip(0.5 + 1.0 * jax.random.uniform(seeds[6], (HEADS,), jnp.float32) ** steps_of(seeds[6], (HEADS,), ((0, 2),), -0.2, 0.2), 0.5, 1.5),
        "norm_gain": jnp.clip(1.0 + 0.15 * jax.random.normal(seeds[7], (CH,), jnp.float32), 0.25, 1.75),
    }


def reference(x_in, gate_in, b_in, c_in, step_size, log_keep, skip_gain, norm_gain):
    block_count = SEQUENCE_TOKENS // BLOCK
    x_blocks = x_in.reshape(block_count, BLOCK, HEADS, HEADDIM)
    b_blocks = b_in.reshape(block_count, BLOCK, STATE)
    c_blocks = c_in.reshape(block_count, BLOCK, STATE)
    keep_blocks = log_keep.reshape(HEADS, block_count, BLOCK).transpose(1, 0, 2)
    step_blocks = step_size.reshape(HEADS, block_count, BLOCK).transpose(1, 0, 2)
    row_index = lax.broadcasted_iota(jnp.int32, (BLOCK, BLOCK), 0)
    col_index = lax.broadcasted_iota(jnp.int32, (BLOCK, BLOCK), 1)
    causal = row_index >= col_index

    def advance(state_now, block_input):
        x_block, b_block, c_block, keep_block, step_block = block_input
        cum_keep = jnp.cumsum(keep_block, axis=1)
        block_total = cum_keep[:, -1]
        scores = jnp.dot(c_block, b_block.T, preferred_element_type=jnp.float32)
        log_gaps = cum_keep[:, :, None] - cum_keep[:, None, :]
        decays = jnp.where(causal[None], jnp.exp(jnp.where(causal[None], log_gaps, 0.0)), 0.0)
        weights = (scores[None] * decays * step_block[:, None, :]).astype(jnp.bfloat16)
        x_float = x_block.astype(jnp.float32)
        output = jnp.einsum('hts,shp->thp', weights.astype(jnp.float32), x_float)
        projected = jnp.einsum('tn,hpn->thp', c_block.astype(jnp.float32), state_now, precision=lax.Precision.HIGHEST)
        output = output + jnp.exp(cum_keep).T[:, :, None] * projected
        decayed_b = ((jnp.exp(block_total[:, None] - cum_keep) * step_block)[:, :, None] * b_block.astype(jnp.float32)[None]).astype(jnp.bfloat16)
        block_state = jnp.einsum('shp,hsn->hpn', x_float, decayed_b.astype(jnp.float32))
        next_state = jnp.exp(block_total)[:, None, None] * state_now + block_state
        return (next_state, output)
    initial = jnp.zeros((HEADS, HEADDIM, STATE), jnp.float32)
    _, outputs = lax.scan(advance, initial, (x_blocks, b_blocks, c_blocks, keep_blocks, step_blocks))
    recurrent = outputs + skip_gain[None, None, :, None] * x_blocks.astype(jnp.float32)
    recurrent = recurrent.reshape(SEQUENCE_TOKENS, CH)
    gated_out = recurrent * jax.nn.silu(gate_in.astype(jnp.float32))
    mean_square = lax.optimization_barrier(jnp.mean(gated_out * gated_out, axis=1))
    return (gated_out * lax.rsqrt(mean_square + 1e-05)[:, None] * norm_gain[None, :]).astype(jnp.bfloat16)
```

```python
import functools

import jax
import jax.numpy as jnp
from jax import lax
from jax.experimental import pallas as pl
from jax.experimental.pallas import tpu as pltpu
from jax.sharding import PartitionSpec as P

BLOCK = 256
SUB = 64
EPSILON = 1e-05
MESH = pl.DeviceIdType.MESH


def dot(a, b, dims):
    return lax.dot_general(a, b, (dims, ((), ())), preferred_element_type=jnp.float32)


def expand(tile, base, head_width, channels):
    lane = lax.broadcasted_iota(jnp.int32, tile.shape, 1)
    pieces = []
    for j in range(channels // 128):
        index = base + (lane + j * 128) // head_width
        pieces.append(jnp.take_along_axis(tile, index, axis=1, mode="promise_in_bounds"))
    return jnp.concatenate(pieces, axis=1)


def decays(log_ref, step_ref, skip_ref, stack, q, spacing):
    heads, tokens = log_ref.shape
    lane = lax.broadcasted_iota(jnp.int32, (heads, tokens), 1)
    pos = lane % SUB
    cum = log_ref[...]
    s = 1
    while s < SUB:
        cum = cum + jnp.where(pos >= s, pltpu.roll(cum, s, 1), 0.0)
        s *= 2
    total = jnp.where(pos == SUB - 1, cum, 0.0)
    s = 1
    while s < SUB:
        total = total + jnp.where(pos < SUB - s, pltpu.roll(total, tokens - s, 1), 0.0)
        s *= 2
    before = jnp.where(lane >= SUB, pltpu.roll(total, SUB, 1), 0.0)
    s = SUB
    while s < tokens:
        before = before + jnp.where(lane >= s, pltpu.roll(before, s, 1), 0.0)
        s *= 2
    mid = 0.5 * total
    stack[...] = jnp.zeros_like(stack)
    stack[0:heads, :] = jnp.exp(mid - cum) * step_ref[...]
    stack[spacing : spacing + heads, :] = jnp.exp(cum - mid)
    stack[2 * spacing : 2 * spacing + heads, :] = jnp.exp(mid)
    stack[3 * spacing : 3 * spacing + heads, :] = jnp.exp(before + mid)
    stack[4 * spacing : 4 * spacing + heads, :] = jnp.broadcast_to(skip_ref[...], (heads, tokens))
    for j in range(tokens // 128):
        q[j * 128 : (j + 1) * 128, :] = jnp.transpose(stack[:, j * 128 : (j + 1) * 128])


def main_kernel(
    n, nchan, spacing,
    x_hbm, gate_hbm, b_ref, c_ref, step_ref, log_ref, skip_ref,
    out_hbm, sq_out,
    x, gate, xs, local, base, es, gated, stack, q, state,
    total_row, totals, give, got, back, entering, sq, sq_got,
    x_sem, gate_sem, out_sem, sems, sq_sems,
):
    tokens, channels = x.shape
    heads = log_ref.shape[0]
    head_width = channels // heads
    nstate = b_ref.shape[1]
    blocks = tokens // BLOCK
    subs = BLOCK // SUB
    rows = nstate // n
    me = lax.axis_index("seq")
    mine = lax.axis_index("chan")

    def block_copy(src, dst, sem, i):
        r = pl.ds(i * BLOCK, BLOCK)
        return pltpu.make_async_copy(src.at[r], dst.at[r], sem.at[i])

    for i in range(blocks):
        block_copy(x_hbm, x, x_sem, i).start()
    for i in range(blocks):
        block_copy(gate_hbm, gate, gate_sem, i).start()

    barrier = pltpu.get_barrier_semaphore()

    @pl.loop(1, n)
    def _(i):
        pl.semaphore_signal(barrier, inc=1, device_id={"seq": lax.rem(me + i, n)}, device_id_type=MESH)

    for i in range(1, nchan):
        pl.semaphore_signal(barrier, inc=1, device_id={"chan": lax.rem(mine + i, nchan)}, device_id_type=MESH)

    def seq_copy(src, dst, kind, to, slot):
        return pltpu.make_async_remote_copy(
            src_ref=src, dst_ref=dst,
            send_sem=sems.at[kind, 0, to], recv_sem=sems.at[kind, 1, slot],
            device_id={"seq": to}, device_id_type=MESH,
        )

    decays(log_ref, step_ref, skip_ref, stack, q, spacing)
    wide = functools.partial(expand, head_width=head_width, channels=channels)
    last = q[tokens - 8 : tokens, :]
    total_row[...] = (wide(last, 2 * spacing) * wide(last, 3 * spacing))[0:1]
    pl.semaphore_wait(barrier, n - 1 + nchan - 1)

    @pl.loop(1, n)
    def _(i):
        to = lax.rem(me + i, n)
        seq_copy(total_row, totals.at[me], 0, to, me).start()

    totals[me] = total_row[...]
    state[...] = jnp.zeros_like(state)

    def times(matrix, row8):
        r, w = matrix.shape
        return (matrix.reshape(r // 8, 8, w) * row8[None]).reshape(r, w)

    @pl.loop(0, blocks)
    def _(i):
        block_copy(x_hbm, x, x_sem, i).wait()
        for j in range(subs):
            start = pl.multiple_of(i * BLOCK + j * SUB, SUB)
            r = pl.ds(start, SUB)
            scaled = (x[r, :].astype(jnp.float32) * wide(q[r, :], 0)).astype(jnp.bfloat16)
            xs[r, :] = scaled
            g = wide(q[pl.ds(start, 8), :], 2 * spacing)
            here = times(state[...], g)
            local[i * subs + j] = here
            state[...] = times(here + dot(b_ref[r, :], scaled, ((0,), (0,))), g)

    for k in range(n):
        give[k] = state[k * rows : (k + 1) * rows, :]

    @pl.loop(1, n)
    def _(i):
        to = lax.rem(me + i, n)
        seq_copy(give.at[to], got.at[me], 1, to, me).start()

    got[me] = give[me]
    skip8 = wide(q[0:8, :], 4 * spacing)
    row = lax.broadcasted_iota(jnp.int32, (SUB, SUB), 0)
    col = lax.broadcasted_iota(jnp.int32, (SUB, SUB), 1)

    def fill(i):
        block_copy(gate_hbm, gate, gate_sem, i).wait()
        for j in range(subs):
            r = pl.ds(pl.multiple_of(i * BLOCK + j * SUB, SUB), SUB)
            scores = dot(c_ref[r, :], b_ref[r, :], ((1,), (1,)))
            scores = jnp.where(row >= col, scores, 0.0).astype(jnp.bfloat16)
            inside = dot(scores, xs[r, :], ((1,), (0,)))
            e2 = wide(q[r, :], spacing)
            half = 0.5 * gate[r, :].astype(jnp.float32)
            silu = half + half * jnp.tanh(half)
            base[r, :] = (e2 * inside + times(x[r, :].astype(jnp.float32), skip8)) * silu
            es[r, :] = e2 * silu

    pl.loop(0, blocks // 2)(fill)

    @pl.loop(1, n)
    def _(i):
        other = lax.rem(me + i, n)
        seq_copy(total_row, totals.at[other], 0, other, other).wait()
        seq_copy(give.at[other], got.at[other], 1, other, other).wait()

    prefix = jnp.zeros((rows, channels), jnp.float32)
    for k in range(n):
        back[k] = prefix
        if k < n - 1:
            prefix = totals[k] * prefix + got[k]

    @pl.loop(1, n)
    def _(i):
        to = lax.rem(me + i, n)
        seq_copy(back.at[to], entering.at[me], 2, to, me).start()

    entering[me] = back[me]
    pl.loop(blocks // 2, blocks)(fill)

    @pl.loop(1, n)
    def _(i):
        other = lax.rem(me + i, n)
        seq_copy(back.at[other], entering.at[other], 2, other, other).wait()

    for k in range(n):
        state[k * rows : (k + 1) * rows, :] = entering[k]

    @pl.loop(0, blocks)
    def _(i):
        sums = []
        for j in range(subs):
            start = pl.multiple_of(i * BLOCK + j * SUB, SUB)
            r = pl.ds(start, SUB)
            g = wide(q[pl.ds(start, 8), :], 3 * spacing)
            here = (local[i * subs + j] + times(state[...], g)).astype(jnp.bfloat16)
            value = base[r, :] + es[r, :] * dot(c_ref[r, :], here, ((1,), (0,)))
            gated[r, :] = value.astype(jnp.bfloat16)
            square = value * value
            part = square[:, 0:128]
            for k in range(1, channels // 128):
                part = part + square[:, k * 128 : (k + 1) * 128]
            sums.append(part)
        for j in range(BLOCK // 128):
            pair = jnp.concatenate(sums[2 * j : 2 * j + 2], axis=0)
            sq[i * (BLOCK // 128) + j] = jnp.sum(jnp.transpose(pair), axis=0, keepdims=True)
        block_copy(gated, out_hbm, out_sem, i).start()

    def chan_copy(to, slot):
        return pltpu.make_async_remote_copy(
            src_ref=sq, dst_ref=sq_got.at[slot],
            send_sem=sq_sems.at[0, to], recv_sem=sq_sems.at[1, slot],
            device_id={"chan": to}, device_id_type=MESH,
        )

    for i in range(1, nchan):
        chan_copy(lax.rem(mine + i, nchan), mine).start()
    sq_got[mine] = sq[...]
    for i in range(blocks):
        block_copy(gated, out_hbm, out_sem, i).wait()
    for i in range(1, nchan):
        other = lax.rem(mine + i, nchan)
        chan_copy(other, other).wait()
    summed = sq_got[0]
    for i in range(1, nchan):
        summed = summed + sq_got[i]
    sq_out[...] = summed


def norm_kernel(total_channels, gated_ref, sq_ref, gain_ref, out_ref):
    channels = gated_ref.shape[1]
    gain = gain_ref[...]
    for j in range(gated_ref.shape[0] // 128):
        factor = lax.rsqrt(sq_ref[j] / total_channels + EPSILON)
        column = jnp.transpose(jnp.broadcast_to(factor, (128, 128)))
        r = slice(j * 128, (j + 1) * 128)
        for k in range(channels // 128):
            w = slice(k * 128, (k + 1) * 128)
            out_ref[r, w] = (gated_ref[r, w].astype(jnp.float32) * column * gain[:, w]).astype(out_ref.dtype)


def per_device(n, nchan, x_in, gate_in, b_in, c_in, step_size, log_keep, skip_gain, norm_gain):
    tokens, channels = x_in.shape
    heads = step_size.shape[0]
    nstate = b_in.shape[1]
    spacing = -(-heads // 8) * 8
    rows = nstate // n
    blocks = tokens // BLOCK
    f32, bf16 = jnp.float32, jnp.bfloat16
    vmem = pl.BlockSpec(memory_space=pltpu.VMEM)
    anywhere = pl.BlockSpec(memory_space=pl.ANY)
    gated, squares = pl.pallas_call(
        functools.partial(main_kernel, n, nchan, spacing),
        out_shape=(
            jax.ShapeDtypeStruct((tokens, channels), bf16),
            jax.ShapeDtypeStruct((tokens // 128, 1, 128), f32),
        ),
        in_specs=[anywhere, anywhere] + [vmem] * 5,
        out_specs=(anywhere, vmem),
        scratch_shapes=[
            pltpu.VMEM((tokens, channels), bf16),
            pltpu.VMEM((tokens, channels), bf16),
            pltpu.VMEM((tokens, channels), bf16),
            pltpu.VMEM((tokens // SUB, nstate, channels), f32),
            pltpu.VMEM((tokens, channels), f32),
            pltpu.VMEM((tokens, channels), f32),
            pltpu.VMEM((tokens, channels), bf16),
            pltpu.VMEM((128, tokens), f32),
            pltpu.VMEM((tokens, 128), f32),
            pltpu.VMEM((nstate, channels), f32),
            pltpu.VMEM((1, channels), f32),
            pltpu.VMEM((n, 1, channels), f32),
            pltpu.VMEM((n, rows, channels), f32),
            pltpu.VMEM((n, rows, channels), f32),
            pltpu.VMEM((n, rows, channels), f32),
            pltpu.VMEM((n, rows, channels), f32),
            pltpu.VMEM((tokens // 128, 1, 128), f32),
            pltpu.VMEM((nchan, tokens // 128, 1, 128), f32),
            pltpu.SemaphoreType.DMA((blocks,)),
            pltpu.SemaphoreType.DMA((blocks,)),
            pltpu.SemaphoreType.DMA((blocks,)),
            pltpu.SemaphoreType.DMA((3, 2, n)),
            pltpu.SemaphoreType.DMA((2, nchan)),
        ],
        compiler_params=pltpu.CompilerParams(
            collective_id=0, has_side_effects=True, vmem_limit_bytes=60 * 2**20
        ),
        name="scan",
    )(x_in, gate_in, b_in, c_in, step_size, log_keep, skip_gain[:, None])
    return pl.pallas_call(
        functools.partial(norm_kernel, channels * nchan),
        grid=(blocks,),
        out_shape=jax.ShapeDtypeStruct((tokens, channels), bf16),
        in_specs=[
            pl.BlockSpec((BLOCK, channels), lambda i: (i, 0)),
            pl.BlockSpec((BLOCK // 128, 1, 128), lambda i: (i, 0, 0)),
            pl.BlockSpec((1, channels), lambda i: (0, 0)),
        ],
        out_specs=pl.BlockSpec((BLOCK, channels), lambda i: (i, 0)),
        compiler_params=pltpu.CompilerParams(dimension_semantics=("arbitrary",)),
        name="norm",
    )(gated, squares, norm_gain[None, :])


def solution(mesh):
    in_specs = (
        P("seq", "chan"),
        P("seq", "chan"),
        P("seq", None),
        P("seq", None),
        P("chan", "seq"),
        P("chan", "seq"),
        P("chan"),
        P("chan"),
    )
    return jax.shard_map(
        functools.partial(per_device, mesh.shape["seq"], mesh.shape["chan"]),
        mesh=mesh,
        in_specs=in_specs,
        out_specs=P("seq", "chan"),
        check_vma=False,
    )
```

```python
import functools

import jax
import jax.numpy as jnp
from jax import lax
from jax.experimental import pallas as pl
from jax.experimental.pallas import tpu as pltpu
from jax.sharding import PartitionSpec as P

BLOCK = 256
SUB = 64
EPSILON = 1e-05
MESH = pl.DeviceIdType.MESH


def dot(a, b, dims):
    return lax.dot_general(a, b, (dims, ((), ())), preferred_element_type=jnp.float32)


def expand(tile, base, head_width, channels):
    lane = lax.broadcasted_iota(jnp.int32, tile.shape, 1)
    pieces = []
    for j in range(channels // 128):
        index = base + (lane + j * 128) // head_width
        pieces.append(jnp.take_along_axis(tile, index, axis=1, mode="promise_in_bounds"))
    return jnp.concatenate(pieces, axis=1)


def decays(log_ref, step_ref, stack, q, spacing):
    heads, tokens = log_ref.shape
    lane = lax.broadcasted_iota(jnp.int32, (heads, tokens), 1)
    pos = lane % SUB
    cum = log_ref[...]
    s = 1
    while s < SUB:
        cum = cum + jnp.where(pos >= s, pltpu.roll(cum, s, 1), 0.0)
        s *= 2
    total = jnp.where(pos == SUB - 1, cum, 0.0)
    s = 1
    while s < SUB:
        total = total + jnp.where(pos < SUB - s, pltpu.roll(total, tokens - s, 1), 0.0)
        s *= 2
    before = jnp.where(lane >= SUB, pltpu.roll(total, SUB, 1), 0.0)
    s = SUB
    while s < tokens:
        before = before + jnp.where(lane >= s, pltpu.roll(before, s, 1), 0.0)
        s *= 2
    mid = 0.5 * total
    stack[...] = jnp.zeros_like(stack)
    stack[0:heads, :] = jnp.exp(mid - cum) * step_ref[...]
    stack[spacing : spacing + heads, :] = jnp.exp(cum - mid)
    stack[2 * spacing : 2 * spacing + heads, :] = jnp.exp(mid)
    stack[3 * spacing : 3 * spacing + heads, :] = jnp.exp(before + mid)
    for j in range(tokens // 128):
        q[j * 128 : (j + 1) * 128, :] = jnp.transpose(stack[:, j * 128 : (j + 1) * 128])


def main_kernel(
    n, nchan, spacing,
    x_hbm, gate_hbm, b_ref, c_ref, step_ref, log_ref, skip_ref,
    base, sq_out,
    x, gate, xs, local, es, c, stack, q, skip_tile, state,
    total_row, totals, give, got, back, entering, sq, sq_got,
    x_sem, gate_sem, sems, sq_sems,
):
    tokens, channels = x.shape
    heads = log_ref.shape[0]
    head_width = channels // heads
    nstate = b_ref.shape[0]
    blocks = tokens // BLOCK
    subs = BLOCK // SUB
    rows = nstate // n
    me = lax.axis_index("seq")
    mine = lax.axis_index("chan")

    def block_copy(src, dst, sem, i):
        r = pl.ds(i * BLOCK, BLOCK)
        return pltpu.make_async_copy(src.at[r], dst.at[r], sem.at[i])

    for i in range(blocks):
        block_copy(x_hbm, x, x_sem, i).start()
    for i in range(blocks):
        block_copy(gate_hbm, gate, gate_sem, i).start()

    barrier = pltpu.get_barrier_semaphore()

    @pl.loop(1, n)
    def _(i):
        pl.semaphore_signal(barrier, inc=1, device_id={"seq": lax.rem(me + i, n)}, device_id_type=MESH)

    for i in range(1, nchan):
        pl.semaphore_signal(barrier, inc=1, device_id={"chan": lax.rem(mine + i, nchan)}, device_id_type=MESH)

    def seq_copy(src, dst, kind, to, slot):
        return pltpu.make_async_remote_copy(
            src_ref=src, dst_ref=dst,
            send_sem=sems.at[kind, 0, to], recv_sem=sems.at[kind, 1, slot],
            device_id={"seq": to}, device_id_type=MESH,
        )

    decays(log_ref, step_ref, stack, q, spacing)
    skip_tile[...] = jnp.zeros_like(skip_tile)
    skip_tile[:, 0:heads] = jnp.broadcast_to(skip_ref[...], (8, heads))
    for j in range(tokens // 128):
        w = slice(j * 128, (j + 1) * 128)
        c[w, :] = jnp.transpose(c_ref[:, w].astype(jnp.float32)).astype(jnp.bfloat16)
    wide = functools.partial(expand, head_width=head_width, channels=channels)
    last = q[tokens - 8 : tokens, :]
    total_row[...] = (wide(last, 2 * spacing) * wide(last, 3 * spacing))[0:1]
    pl.semaphore_wait(barrier, n - 1 + nchan - 1)

    @pl.loop(1, n)
    def _(i):
        to = lax.rem(me + i, n)
        seq_copy(total_row, totals.at[me], 0, to, me).start()

    totals[me] = total_row[...]
    state[...] = jnp.zeros_like(state)

    def b_sub(i, j):
        pair = b_ref[:, pl.ds(pl.multiple_of(i * BLOCK + j // 2 * 128, 128), 128)]
        return pair[:, j % 2 * SUB : (j % 2 + 1) * SUB]

    def times(matrix, row8):
        r, w = matrix.shape
        return (matrix.reshape(r // 8, 8, w) * row8[None]).reshape(r, w)

    @pl.loop(0, blocks)
    def _(i):
        block_copy(x_hbm, x, x_sem, i).wait()
        for j in range(subs):
            start = pl.multiple_of(i * BLOCK + j * SUB, SUB)
            r = pl.ds(start, SUB)
            scaled = (x[r, :].astype(jnp.float32) * wide(q[r, :], 0)).astype(jnp.bfloat16)
            xs[r, :] = scaled
            g = wide(q[pl.ds(start, 8), :], 2 * spacing)
            here = times(state[...], g)
            local[i * subs + j] = here
            state[...] = times(here + dot(b_sub(i, j), scaled, ((1,), (0,))), g)

    for k in range(n):
        give[k] = state[k * rows : (k + 1) * rows, :]

    @pl.loop(1, n)
    def _(i):
        to = lax.rem(me + i, n)
        seq_copy(give.at[to], got.at[me], 1, to, me).start()

    got[me] = give[me]
    skip8 = wide(skip_tile[...], 0)
    row = lax.broadcasted_iota(jnp.int32, (SUB, SUB), 0)
    col = lax.broadcasted_iota(jnp.int32, (SUB, SUB), 1)

    def fill(i):
        block_copy(gate_hbm, gate, gate_sem, i).wait()
        for j in range(subs):
            r = pl.ds(pl.multiple_of(i * BLOCK + j * SUB, SUB), SUB)
            scores = dot(c[r, :], b_sub(i, j), ((1,), (0,)))
            scores = jnp.where(row >= col, scores, 0.0).astype(jnp.bfloat16)
            inside = dot(scores, xs[r, :], ((1,), (0,)))
            e2 = wide(q[r, :], spacing)
            half = 0.5 * gate[r, :].astype(jnp.float32)
            silu = half + half * jnp.tanh(half)
            base[r, :] = (e2 * inside + times(x[r, :].astype(jnp.float32), skip8)) * silu
            es[r, :] = e2 * silu

    pl.loop(0, blocks // 2)(fill)

    @pl.loop(1, n)
    def _(i):
        other = lax.rem(me + i, n)
        seq_copy(total_row, totals.at[other], 0, other, other).wait()
        seq_copy(give.at[other], got.at[other], 1, other, other).wait()

    prefix = jnp.zeros((rows, channels), jnp.float32)
    for k in range(n):
        back[k] = prefix
        if k < n - 1:
            prefix = totals[k] * prefix + got[k]

    @pl.loop(1, n)
    def _(i):
        to = lax.rem(me + i, n)
        seq_copy(back.at[to], entering.at[me], 2, to, me).start()

    entering[me] = back[me]
    pl.loop(blocks // 2, blocks)(fill)

    @pl.loop(1, n)
    def _(i):
        other = lax.rem(me + i, n)
        seq_copy(back.at[other], entering.at[other], 2, other, other).wait()

    for k in range(n):
        state[k * rows : (k + 1) * rows, :] = entering[k]

    @pl.loop(0, blocks)
    def _(i):
        sums = []
        for j in range(subs):
            start = pl.multiple_of(i * BLOCK + j * SUB, SUB)
            r = pl.ds(start, SUB)
            g = wide(q[pl.ds(start, 8), :], 3 * spacing)
            here = (local[i * subs + j] + times(state[...], g)).astype(jnp.bfloat16)
            value = base[r, :] + es[r, :] * dot(c[r, :], here, ((1,), (0,)))
            base[r, :] = value
            square = value * value
            part = square[:, 0:128]
            for k in range(1, channels // 128):
                part = part + square[:, k * 128 : (k + 1) * 128]
            sums.append(part)
        for j in range(BLOCK // 128):
            pair = jnp.concatenate(sums[2 * j : 2 * j + 2], axis=0)
            sq[i * (BLOCK // 128) + j] = jnp.sum(jnp.transpose(pair), axis=0, keepdims=True)

    def chan_copy(to, slot):
        return pltpu.make_async_remote_copy(
            src_ref=sq, dst_ref=sq_got.at[slot],
            send_sem=sq_sems.at[0, to], recv_sem=sq_sems.at[1, slot],
            device_id={"chan": to}, device_id_type=MESH,
        )

    for i in range(1, nchan):
        chan_copy(lax.rem(mine + i, nchan), mine).start()
    sq_got[mine] = sq[...]
    for i in range(1, nchan):
        other = lax.rem(mine + i, nchan)
        chan_copy(other, other).wait()
    summed = sq_got[0]
    for i in range(1, nchan):
        summed = summed + sq_got[i]
    sq_out[...] = summed


def norm_kernel(total_channels, gated, sq_ref, gain_ref, out_hbm, out, sem):
    tokens, channels = gated.shape

    def copy(i):
        r = pl.ds(i * BLOCK, BLOCK)
        return pltpu.make_async_copy(out.at[r], out_hbm.at[r], sem.at[i])

    @pl.loop(0, tokens // BLOCK)
    def _(i):
        gain = gain_ref[...]
        for j in range(BLOCK // 128):
            factor = lax.rsqrt(sq_ref[i * (BLOCK // 128) + j] / total_channels + EPSILON)
            column = jnp.transpose(jnp.broadcast_to(factor, (128, 128)))
            r = pl.ds(pl.multiple_of(i * BLOCK + j * 128, 128), 128)
            for k in range(channels // 128):
                w = slice(k * 128, (k + 1) * 128)
                out[r, w] = (gated[r, w] * column * gain[:, w]).astype(out.dtype)
        copy(i).start()

    for i in range(tokens // BLOCK):
        copy(i).wait()


def per_device(n, nchan, x_in, gate_in, b_in, c_in, step_size, log_keep, skip_gain, norm_gain):
    tokens, channels = x_in.shape
    heads = step_size.shape[0]
    nstate = b_in.shape[1]
    spacing = -(-heads // 8) * 8
    rows = nstate // n
    blocks = tokens // BLOCK
    f32, bf16 = jnp.float32, jnp.bfloat16
    vmem = pl.BlockSpec(memory_space=pltpu.VMEM)
    anywhere = pl.BlockSpec(memory_space=pltpu.HBM)
    gated, squares = pl.pallas_call(
        functools.partial(main_kernel, n, nchan, spacing),
        out_shape=(
            pltpu.VMEM((tokens, channels), f32),
            jax.ShapeDtypeStruct((tokens // 128, 1, 128), f32),
        ),
        in_specs=[anywhere, anywhere] + [vmem] * 5,
        out_specs=(vmem, vmem),
        scratch_shapes=[
            pltpu.VMEM((tokens, channels), bf16),
            pltpu.VMEM((tokens, channels), bf16),
            pltpu.VMEM((tokens, channels), bf16),
            pltpu.VMEM((tokens // SUB, nstate, channels), f32),
            pltpu.VMEM((tokens, channels), f32),
            pltpu.VMEM((tokens, nstate), bf16),
            pltpu.VMEM((128, tokens), f32),
            pltpu.VMEM((tokens, 128), f32),
            pltpu.VMEM((8, 128), f32),
            pltpu.VMEM((nstate, channels), f32),
            pltpu.VMEM((1, channels), f32),
            pltpu.VMEM((n, 1, channels), f32),
            pltpu.VMEM((n, rows, channels), f32),
            pltpu.VMEM((n, rows, channels), f32),
            pltpu.VMEM((n, rows, channels), f32),
            pltpu.VMEM((n, rows, channels), f32),
            pltpu.VMEM((tokens // 128, 1, 128), f32),
            pltpu.VMEM((nchan, tokens // 128, 1, 128), f32),
            pltpu.SemaphoreType.DMA((blocks,)),
            pltpu.SemaphoreType.DMA((blocks,)),
            pltpu.SemaphoreType.DMA((3, 2, n)),
            pltpu.SemaphoreType.DMA((2, nchan)),
        ],
        compiler_params=pltpu.CompilerParams(
            collective_id=0, has_side_effects=True, vmem_limit_bytes=50 * 2**20
        ),
        name="scan",
    )(x_in, gate_in, b_in.T, c_in.T, step_size, log_keep, skip_gain[None, :])
    return pl.pallas_call(
        functools.partial(norm_kernel, channels * nchan),
        out_shape=jax.ShapeDtypeStruct((tokens, channels), bf16),
        in_specs=[vmem] * 3,
        out_specs=anywhere,
        scratch_shapes=[pltpu.VMEM((tokens, channels), bf16), pltpu.SemaphoreType.DMA((blocks,))],
        compiler_params=pltpu.CompilerParams(vmem_limit_bytes=16 * 2**20),
        name="norm",
    )(gated, squares, norm_gain[None, :])


def solution(mesh):
    in_specs = (
        P("seq", "chan"),
        P("seq", "chan"),
        P("seq", None),
        P("seq", None),
        P("chan", "seq"),
        P("chan", "seq"),
        P("chan"),
        P("chan"),
    )
    return jax.shard_map(
        functools.partial(per_device, mesh.shape["seq"], mesh.shape["chan"]),
        mesh=mesh,
        in_specs=in_specs,
        out_specs=P("seq", "chan"),
        check_vma=False,
    )
```

```python
import functools

import jax
import jax.numpy as jnp
from jax import lax
from jax.experimental import pallas as pl
from jax.experimental.pallas import tpu as pltpu
from jax.sharding import PartitionSpec as P

BLOCK = 256
SUB = 64
EPSILON = 1e-05
MESH = pl.DeviceIdType.MESH


def dot(a, b, dims):
    return lax.dot_general(a, b, (dims, ((), ())), preferred_element_type=jnp.float32)


def expand(tile, base, head_width, channels):
    lane = lax.broadcasted_iota(jnp.int32, tile.shape, 1)
    pieces = []
    for j in range(channels // 128):
        index = base + (lane + j * 128) // head_width
        pieces.append(jnp.take_along_axis(tile, index, axis=1, mode="promise_in_bounds"))
    return jnp.concatenate(pieces, axis=1)


def decays(log_ref, step_ref, stack, q, spacing):
    heads, tokens = log_ref.shape
    lane = lax.broadcasted_iota(jnp.int32, (heads, tokens), 1)
    pos = lane % SUB
    cum = log_ref[...]
    s = 1
    while s < SUB:
        cum = cum + jnp.where(pos >= s, pltpu.roll(cum, s, 1), 0.0)
        s *= 2
    total = jnp.where(pos == SUB - 1, cum, 0.0)
    s = 1
    while s < SUB:
        total = total + jnp.where(pos < SUB - s, pltpu.roll(total, tokens - s, 1), 0.0)
        s *= 2
    before = jnp.where(lane >= SUB, pltpu.roll(total, SUB, 1), 0.0)
    s = SUB
    while s < tokens:
        before = before + jnp.where(lane >= s, pltpu.roll(before, s, 1), 0.0)
        s *= 2
    mid = 0.5 * total
    stack[...] = jnp.zeros_like(stack)
    stack[0:heads, :] = jnp.exp(mid - cum) * step_ref[...]
    stack[spacing : spacing + heads, :] = jnp.exp(cum - mid)
    stack[2 * spacing : 2 * spacing + heads, :] = jnp.exp(mid)
    stack[3 * spacing : 3 * spacing + heads, :] = jnp.exp(before + mid)
    for j in range(tokens // 128):
        q[j * 128 : (j + 1) * 128, :] = jnp.transpose(stack[:, j * 128 : (j + 1) * 128])


def main_kernel(
    n, nchan, spacing,
    x_hbm, gate_hbm, b_ref, c_ref, step_ref, log_ref, skip_ref,
    base, sq_out,
    x, gate, xs, local, es, c, stack, q, skip_tile, state,
    total_row, totals, give, got, back, entering, low_total, low_got, sq, sq_got,
    x_sem, gate_sem, sems, hop_sems, sq_sems,
):
    tokens, channels = x.shape
    heads = log_ref.shape[0]
    head_width = channels // heads
    nstate = b_ref.shape[0]
    blocks = tokens // BLOCK
    subs = BLOCK // SUB
    rows = nstate // (n // 2)
    me = lax.axis_index("seq")
    mine = lax.axis_index("chan")

    def block_copy(src, dst, sem, i):
        r = pl.ds(i * BLOCK, BLOCK)
        return pltpu.make_async_copy(src.at[r], dst.at[r], sem.at[i])

    for i in range(blocks):
        block_copy(x_hbm, x, x_sem, i).start()
    for i in range(blocks):
        block_copy(gate_hbm, gate, gate_sem, i).start()

    group = n // 2
    half, place = me // group, lax.rem(me, group)
    across = lax.rem(me + group, n)

    def peer(i):
        slot = lax.rem(place + i, group)
        return slot, half * group + slot

    barrier = pltpu.get_barrier_semaphore()

    @pl.loop(1, group)
    def _(i):
        pl.semaphore_signal(barrier, inc=1, device_id={"seq": peer(i)[1]}, device_id_type=MESH)

    pl.semaphore_signal(barrier, inc=1, device_id={"seq": across}, device_id_type=MESH)

    for i in range(1, nchan):
        pl.semaphore_signal(barrier, inc=1, device_id={"chan": lax.rem(mine + i, nchan)}, device_id_type=MESH)

    def seq_copy(src, dst, kind, i, slot):
        give_slot, to = peer(i)
        return pltpu.make_async_remote_copy(
            src_ref=src, dst_ref=dst,
            send_sem=sems.at[kind, 0, give_slot], recv_sem=sems.at[kind, 1, slot],
            device_id={"seq": to}, device_id_type=MESH,
        )

    decays(log_ref, step_ref, stack, q, spacing)
    skip_tile[...] = jnp.zeros_like(skip_tile)
    skip_tile[:, 0:heads] = jnp.broadcast_to(skip_ref[...], (8, heads))
    for j in range(tokens // 128):
        w = slice(j * 128, (j + 1) * 128)
        c[w, :] = jnp.transpose(c_ref[:, w].astype(jnp.float32)).astype(jnp.bfloat16)
    wide = functools.partial(expand, head_width=head_width, channels=channels)
    last = q[tokens - 8 : tokens, :]
    total_row[...] = (wide(last, 2 * spacing) * wide(last, 3 * spacing))[0:1]
    state[...] = jnp.zeros_like(state)

    def b_sub(i, j):
        pair = b_ref[:, pl.ds(pl.multiple_of(i * BLOCK + j // 2 * 128, 128), 128)]
        return pair[:, j % 2 * SUB : (j % 2 + 1) * SUB]

    def times(matrix, row8):
        r, w = matrix.shape
        return (matrix.reshape(r // 8, 8, w) * row8[None]).reshape(r, w)

    @pl.loop(0, blocks)
    def _(i):
        block_copy(x_hbm, x, x_sem, i).wait()
        for j in range(subs):
            start = pl.multiple_of(i * BLOCK + j * SUB, SUB)
            r = pl.ds(start, SUB)
            scaled = (x[r, :].astype(jnp.float32) * wide(q[r, :], 0)).astype(jnp.bfloat16)
            xs[r, :] = scaled
            g = wide(q[pl.ds(start, 8), :], 2 * spacing)
            here = times(state[...], g)
            local[i * subs + j] = here
            state[...] = times(here + dot(b_sub(i, j), scaled, ((1,), (0,))), g)

    for k in range(group):
        give[k] = state[k * rows : (k + 1) * rows, :]
    pl.semaphore_wait(barrier, group + nchan - 1)

    @pl.loop(1, group)
    def _(i):
        seq_copy(give.at[peer(i)[0]], got.at[place], 1, i, place).start()
        seq_copy(total_row, totals.at[place], 0, i, place).start()

    got[place] = give[place]
    totals[place] = total_row[...]
    skip8 = wide(skip_tile[...], 0)
    row = lax.broadcasted_iota(jnp.int32, (SUB, SUB), 0)
    col = lax.broadcasted_iota(jnp.int32, (SUB, SUB), 1)

    def fill(i):
        block_copy(gate_hbm, gate, gate_sem, i).wait()
        for j in range(subs):
            r = pl.ds(pl.multiple_of(i * BLOCK + j * SUB, SUB), SUB)
            scores = dot(c[r, :], b_sub(i, j), ((1,), (0,)))
            scores = jnp.where(row >= col, scores, 0.0).astype(jnp.bfloat16)
            inside = dot(scores, xs[r, :], ((1,), (0,)))
            e2 = wide(q[r, :], spacing)
            half = 0.5 * gate[r, :].astype(jnp.float32)
            silu = half + half * jnp.tanh(half)
            base[r, :] = (e2 * inside + times(x[r, :].astype(jnp.float32), skip8)) * silu
            es[r, :] = e2 * silu

    first, second = blocks * 4 // 8, blocks * 5 // 8
    pl.loop(0, first)(fill)

    @pl.loop(1, group)
    def _(i):
        slot = peer(i)[0]
        seq_copy(give.at[slot], got.at[slot], 1, i, slot).wait()
        seq_copy(total_row, totals.at[slot], 0, i, slot).wait()

    hop = pltpu.make_async_remote_copy(
        src_ref=low_total, dst_ref=low_got, send_sem=hop_sems.at[0], recv_sem=hop_sems.at[1],
        device_id={"seq": across}, device_id_type=MESH,
    )

    def run(prefix):
        for k in range(group):
            back[k] = prefix
            prefix = totals[k] * prefix + got[k]
        return prefix

    def send_back():
        @pl.loop(1, group)
        def _(i):
            seq_copy(back.at[peer(i)[0]], entering.at[place], 2, i, place).start()

        entering[place] = back[place]

    @pl.when(half == 0)
    def _():
        low_total[...] = run(jnp.zeros((rows, channels), jnp.float32))
        hop.start()
        send_back()

    pl.loop(first, second)(fill)

    @pl.when(half == 1)
    def _():
        hop.wait_recv()
        run(low_got[...])
        send_back()

    pl.loop(second, blocks)(fill)

    @pl.loop(1, group)
    def _(i):
        slot = peer(i)[0]
        seq_copy(back.at[slot], entering.at[slot], 2, i, slot).wait()

    @pl.when(half == 0)
    def _():
        hop.wait_send()

    for k in range(group):
        state[k * rows : (k + 1) * rows, :] = entering[k]

    @pl.loop(0, blocks)
    def _(i):
        sums = []
        for j in range(subs):
            start = pl.multiple_of(i * BLOCK + j * SUB, SUB)
            r = pl.ds(start, SUB)
            g = wide(q[pl.ds(start, 8), :], 3 * spacing)
            here = (local[i * subs + j] + times(state[...], g)).astype(jnp.bfloat16)
            value = base[r, :] + es[r, :] * dot(c[r, :], here, ((1,), (0,)))
            base[r, :] = value
            square = value * value
            part = square[:, 0:128]
            for k in range(1, channels // 128):
                part = part + square[:, k * 128 : (k + 1) * 128]
            sums.append(part)
        for j in range(BLOCK // 128):
            pair = jnp.concatenate(sums[2 * j : 2 * j + 2], axis=0)
            sq[i * (BLOCK // 128) + j] = jnp.sum(jnp.transpose(pair), axis=0, keepdims=True)

    def chan_copy(to, slot):
        return pltpu.make_async_remote_copy(
            src_ref=sq, dst_ref=sq_got.at[slot],
            send_sem=sq_sems.at[0, to], recv_sem=sq_sems.at[1, slot],
            device_id={"chan": to}, device_id_type=MESH,
        )

    for i in range(1, nchan):
        chan_copy(lax.rem(mine + i, nchan), mine).start()
    sq_got[mine] = sq[...]
    for i in range(1, nchan):
        other = lax.rem(mine + i, nchan)
        chan_copy(other, other).wait()
    summed = sq_got[0]
    for i in range(1, nchan):
        summed = summed + sq_got[i]
    sq_out[...] = summed


def norm_kernel(total_channels, gated, sq_ref, gain_ref, out_hbm, out, sem):
    tokens, channels = gated.shape

    def copy(i):
        r = pl.ds(i * BLOCK, BLOCK)
        return pltpu.make_async_copy(out.at[r], out_hbm.at[r], sem.at[i])

    @pl.loop(0, tokens // BLOCK)
    def _(i):
        gain = gain_ref[...]
        for j in range(BLOCK // 128):
            factor = lax.rsqrt(sq_ref[i * (BLOCK // 128) + j] / total_channels + EPSILON)
            column = jnp.transpose(jnp.broadcast_to(factor, (128, 128)))
            r = pl.ds(pl.multiple_of(i * BLOCK + j * 128, 128), 128)
            for k in range(channels // 128):
                w = slice(k * 128, (k + 1) * 128)
                out[r, w] = (gated[r, w] * column * gain[:, w]).astype(out.dtype)
        copy(i).start()

    for i in range(tokens // BLOCK):
        copy(i).wait()


def per_device(n, nchan, x_in, gate_in, b_in, c_in, step_size, log_keep, skip_gain, norm_gain):
    tokens, channels = x_in.shape
    heads = step_size.shape[0]
    nstate = b_in.shape[1]
    spacing = -(-heads // 8) * 8
    group = n // 2
    rows = nstate // group
    blocks = tokens // BLOCK
    f32, bf16 = jnp.float32, jnp.bfloat16
    vmem = pl.BlockSpec(memory_space=pltpu.VMEM)
    anywhere = pl.BlockSpec(memory_space=pltpu.HBM)
    gated, squares = pl.pallas_call(
        functools.partial(main_kernel, n, nchan, spacing),
        out_shape=(
            pltpu.VMEM((tokens, channels), f32),
            pltpu.VMEM((tokens // 128, 1, 128), f32),
        ),
        in_specs=[anywhere, anywhere] + [vmem] * 5,
        out_specs=(vmem, vmem),
        scratch_shapes=[
            pltpu.VMEM((tokens, channels), bf16),
            pltpu.VMEM((tokens, channels), bf16),
            pltpu.VMEM((tokens, channels), bf16),
            pltpu.VMEM((tokens // SUB, nstate, channels), f32),
            pltpu.VMEM((tokens, channels), f32),
            pltpu.VMEM((tokens, nstate), bf16),
            pltpu.VMEM((128, tokens), f32),
            pltpu.VMEM((tokens, 128), f32),
            pltpu.VMEM((8, 128), f32),
            pltpu.VMEM((nstate, channels), f32),
            pltpu.VMEM((1, channels), f32),
            pltpu.VMEM((group, 1, channels), f32),
            pltpu.VMEM((group, rows, channels), f32),
            pltpu.VMEM((group, rows, channels), f32),
            pltpu.VMEM((group, rows, channels), f32),
            pltpu.VMEM((group, rows, channels), f32),
            pltpu.VMEM((rows, channels), f32),
            pltpu.VMEM((rows, channels), f32),
            pltpu.VMEM((tokens // 128, 1, 128), f32),
            pltpu.VMEM((nchan, tokens // 128, 1, 128), f32),
            pltpu.SemaphoreType.DMA((blocks,)),
            pltpu.SemaphoreType.DMA((blocks,)),
            pltpu.SemaphoreType.DMA((3, 2, group)),
            pltpu.SemaphoreType.DMA((2,)),
            pltpu.SemaphoreType.DMA((2, nchan)),
        ],
        compiler_params=pltpu.CompilerParams(
            collective_id=0, has_side_effects=True, vmem_limit_bytes=50 * 2**20
        ),
        name="scan",
    )(x_in, gate_in, b_in.T, c_in.T, step_size, log_keep, skip_gain[None, :])
    return pl.pallas_call(
        functools.partial(norm_kernel, channels * nchan),
        out_shape=jax.ShapeDtypeStruct((tokens, channels), bf16),
        in_specs=[vmem] * 3,
        out_specs=anywhere,
        scratch_shapes=[pltpu.VMEM((tokens, channels), bf16), pltpu.SemaphoreType.DMA((blocks,))],
        compiler_params=pltpu.CompilerParams(vmem_limit_bytes=16 * 2**20),
        name="norm",
    )(gated, squares, norm_gain[None, :])


def solution(mesh):
    in_specs = (
        P("seq", "chan"),
        P("seq", "chan"),
        P("seq", None),
        P("seq", None),
        P("chan", "seq"),
        P("chan", "seq"),
        P("chan"),
        P("chan"),
    )
    return jax.shard_map(
        functools.partial(per_device, mesh.shape["seq"], mesh.shape["chan"]),
        mesh=mesh,
        in_specs=in_specs,
        out_specs=P("seq", "chan"),
        check_vma=False,
    )
```
